32 devices in a mesh: src: 16 (over z, y, core), tgt: 2 (over x).
Axes of the slice: x: 2, y: 2, z: 4, core: 2. Of those that a mesh axis runs over, the one named last changes fastest.
Arguments:
- inputs: bfloat16 [64, 2, 1024, 512], P(('src', 'tgt')), may hold values from -6 to 6
- leaf_maps: bfloat16 [64, 2, 256, 1024], P(('src', 'tgt')), may hold values from -0.125 to 0.125
- transfer_blocks: bfloat16 [4, 64, 2, 2, 256, 256], P(None, ('src', 'tgt')), may hold values from -0.1875 to 0.1875
Outputs:
- butterfly_out: bfloat16 [64, 2, 256, 512], P(('src', 'tgt'))
The draws below stay inside these ranges and needn't reach their ends.
All inputs are finite; a program needn't handle non-finite values.
Results may differ from the reference program's by a relative error of at most 0.012.
Values may be sent and summed in bfloat16 or wider, within the bound.
A program may use at most 64 MiB of HBM per device.

```python
import jax
import jax.numpy as jnp
from jax import lax

M = 1024
K = 256
R = 512
LEVELS = 4
LEAVES = 64
N_TGT = 2


def level_of(rng, extent, shards, smallest, high):
    def one(position, shards_of):
        heights = jax.random.uniform(jax.random.fold_in(jax.random.fold_in(rng, 6), position), (shards_of,), jnp.float32, smallest / len(shards), high / len(shards))
        return jnp.repeat(jnp.exp(heights), extent[position] // shards_of).reshape((-1,) + (1,) * (len(extent) - position - 1))

    factor_of = one(*shards[0])
    for cut in shards[1:]:
        factor_of = factor_of * one(*cut)
    return factor_of


def normal_values(rng, shape, deviation, bound, split=(), kind=jnp.bfloat16):
    level = level_of(rng, shape, split, -0.22, 0.18) if split else 1.0
    entries = jax.random.normal(rng, shape, jnp.float32) * deviation * level
    return jnp.minimum(jnp.maximum(entries, -bound), bound).astype(kind)


def setup_inputs(seed: int = 0) -> dict:
    seeds = jax.random.split(jax.random.key(seed), 4)
    return {
        "inputs": normal_values(seeds[0], (LEAVES, 2, M, R), 1.0, 6.0, ((0, 32),)),
        "leaf_maps": normal_values(seeds[1], (LEAVES, 2, K, M), (2 * M) ** -0.5, 0.125, ((0, 32),)),
        "transfer_blocks": normal_values(seeds[2], (LEVELS, LEAVES, 2, 2, K, K), (4 * K) ** -0.5, 0.1875, ((1, 32),)),
    }


def complex_product(blocks, vectors):
    real_part = jnp.dot(blocks[0], vectors[0], preferred_element_type=jnp.float32) - jnp.dot(blocks[1], vectors[1], preferred_element_type=jnp.float32)
    imag_part = jnp.dot(blocks[0], vectors[1], preferred_element_type=jnp.float32) + jnp.dot(blocks[1], vectors[0], preferred_element_type=jnp.float32)
    return jnp.stack([real_part, imag_part])


def butterfly_level(coeffs, blocks, stride):
    groups = LEAVES // (2 * stride)
    paired = coeffs.reshape(groups, 2, stride, 2, K, R).transpose(0, 2, 1, 3, 4, 5).reshape(groups * stride, 2, 2, K, R)
    block_pairs = blocks.reshape(groups, 2, stride, 2, 2, K, K).transpose(0, 2, 1, 3, 4, 5, 6).reshape(groups * stride, 2, 2, 2, K, K)

    def combine_pair(pair_items):
        vectors, pair_blocks = pair_items
        halves = []
        for target_bit in range(2):
            own_term = complex_product(pair_blocks[target_bit, target_bit], vectors[target_bit])
            partner = complex_product(pair_blocks[1 - target_bit, target_bit], vectors[1 - target_bit]).astype(jnp.bfloat16)
            halves.append(own_term + partner.astype(jnp.float32))
        return jnp.stack(halves).astype(jnp.bfloat16)

    updated = lax.map(combine_pair, (paired, block_pairs))
    return updated.reshape(groups, stride, 2, 2, K, R).transpose(0, 2, 1, 3, 4, 5).reshape(LEAVES, 2, K, R)


def reference(inputs, leaf_maps, transfer_blocks):
    coeffs = lax.map(lambda pair_items: complex_product(pair_items[0], pair_items[1]).astype(jnp.bfloat16), (leaf_maps, inputs))
    for level_index, stride in enumerate((1, LEAVES // 2, LEAVES // 4, N_TGT)):
        coeffs = butterfly_level(coeffs, transfer_blocks[level_index], stride)
    return coeffs
```

```python
import functools

import jax
import jax.numpy as jnp
from jax import lax
from jax.experimental import pallas as pl
from jax.experimental.pallas import tpu as pltpu
from jax.sharding import PartitionSpec as P

MESH = pl.DeviceIdType.MESH
LANES = 128
LAG = 2


def product(blocks, vectors):
    rows = blocks.shape[0] // 2
    width = vectors.shape[1] // 2
    both = jnp.dot(blocks, vectors, preferred_element_type=jnp.float32)
    real_part = both[:rows, :width] - both[rows:, width:]
    imag_part = both[:rows, width:] + both[rows:, :width]
    return jnp.concatenate([real_part, imag_part], axis=1)


def kernel(
    sizes,
    inputs,
    leaf_maps,
    transfer,
    out,
    x_in,
    maps,
    blocks,
    coeffs,
    local_term,
    send1,
    recv1,
    send2,
    recv2,
    send3,
    recv3,
    result,
    in_sem,
    maps_sem,
    blocks_sem,
    out_sem,
    s1_sem,
    r1_sem,
    s2_sem,
    r2_sem,
    s3_sem,
    r3_sem,
):
    src_bits, tgt_bits, levels, chunks = sizes
    units = 2 * chunks
    src, tgt = lax.axis_index("src"), lax.axis_index("tgt")
    hi, lo = 2 ** (src_bits - 1), 2 ** (src_bits - 2)
    far = 2 ** (tgt_bits - 1)
    bit1, bit2, bit3 = src // hi % 2, src // lo % 2, tgt // far % 2
    across = (src + hi - 2 * hi * bit1, tgt)
    near = (src + lo - 2 * lo * bit2, tgt)
    side = (src, tgt + far - 2 * far * bit3)
    is_end = bit1 == bit2
    is_mid = bit1 != bit2

    barrier = pltpu.get_barrier_semaphore()
    for peer in (across, near, side):
        pl.semaphore_signal(barrier, inc=1, device_id=peer, device_id_type=MESH)

    def load_in(c, n, part):
        return pltpu.make_async_copy(
            inputs.at[n, part, :, pl.ds(pl.multiple_of(c * LANES, LANES), LANES)],
            x_in.at[c, n, :, pl.ds(part * LANES, LANES)],
            in_sem.at[c, n, part],
        )

    def load_maps(n):
        return pltpu.make_async_copy(leaf_maps.at[n], maps.at[n], maps_sem.at[n])

    def load_blocks(v):
        return pltpu.make_async_copy(transfer.at[v], blocks.at[v], blocks_sem.at[v])

    for n in range(2):
        load_maps(n).start()
        for part in range(2):
            load_in(0, n, part).start()
    load_blocks(0).start()
    load_blocks(1).start()
    for c in range(1, chunks):
        for n in range(2):
            for part in range(2):
                load_in(c, n, part).start()
    for v in range(2, levels):
        load_blocks(v).start()

    def remote(source, target, send_sem, recv_sem, peer):
        return pltpu.make_async_remote_copy(
            src_ref=source,
            dst_ref=target,
            send_sem=send_sem,
            recv_sem=recv_sem,
            device_id=peer,
            device_id_type=MESH,
        )

    def first(u):
        return remote(send1.at[u], recv1.at[u], s1_sem.at[u], r1_sem.at[u], across)

    def second(u):
        return remote(send2.at[u], recv2.at[u], s2_sem.at[u], r2_sem.at[u], near)

    def third(u):
        return remote(send3.at[u], recv3.at[u], s3_sem.at[u], r3_sem.at[u], side)

    def store(u, part):
        return pltpu.make_async_copy(
            result.at[u, :, pl.ds(part * LANES, LANES)],
            out.at[u % 2, part, :, pl.ds(pl.multiple_of(u // 2 * LANES, LANES), LANES)],
            out_sem.at[u, part],
        )

    def pre(c):
        vectors = []
        for n in range(2):
            for part in range(2):
                load_in(c, n, part).wait()
            vectors.append(product(maps[n], x_in[c, n]).astype(jnp.bfloat16))

        @pl.when(c == 0)
        def _():
            load_blocks(0).wait()
            load_blocks(1).wait()

        for n in range(2):
            own_term = product(blocks[0, n, n], vectors[n])
            partner = product(blocks[0, 1 - n, n], vectors[1 - n]).astype(jnp.bfloat16)
            updated = (own_term + partner.astype(jnp.float32)).astype(jnp.bfloat16)
            u = 2 * c + n
            coeffs[u] = updated
            send1[u] = product(blocks[1, n, 1 - bit1], updated).astype(jnp.bfloat16)
            if n == 0:

                @pl.when(c == 0)
                def _():
                    pl.semaphore_wait(barrier, 3)

            first(u).start()

    def plus(local_value, arrived):
        return (local_value + arrived.astype(jnp.float32)).astype(jnp.bfloat16)

    def finish1(u, updated):
        send2[u] = product(blocks[2, u % 2, 1 - bit2], updated).astype(jnp.bfloat16)
        second(u).start()
        return product(blocks[2, u % 2, bit2], updated)

    def finish2(u, local_value):
        second(u).wait_recv()
        updated = plus(local_value, recv2[u])
        send3[u] = product(blocks[3, u % 2, 1 - bit3], updated).astype(jnp.bfloat16)
        third(u).start()
        local_term[u] = product(blocks[3, u % 2, bit3], updated)

    for n in range(2):
        load_maps(n).wait()

    @pl.loop(0, chunks)
    def _(c):
        pre(c)

    for v in range(2, levels):
        load_blocks(v).wait()

    @pl.when(is_end)
    def _():
        @pl.loop(0, units)
        def _(u):
            local_term[u] = product(blocks[1, u % 2, bit1], coeffs[u])

    @pl.when(is_mid)
    def _():
        @pl.loop(0, units)
        def _(u):
            local_value = product(blocks[1, u % 2, bit1], coeffs[u])
            first(u).wait_recv()
            local_term[u] = finish1(u, plus(local_value, recv1[u]))

    @pl.loop(0, units + LAG)
    def _(u):
        @pl.when(jnp.logical_and(is_end, u < units))
        def _():
            first(u).wait_recv()
            finish2(u, finish1(u, plus(local_term[u], recv1[u])))

        @pl.when(jnp.logical_and(is_mid, u < units))
        def _():
            finish2(u, local_term[u])

        @pl.when(u >= LAG)
        def _():
            w = u - LAG
            third(w).wait_recv()
            result[w] = plus(local_term[w], recv3[w])
            for part in range(2):
                store(w, part).start()

    @pl.loop(0, units)
    def _(u):
        first(u).wait_send()
        second(u).wait_send()
        third(u).wait_send()
        for part in range(2):
            store(u, part).wait()


def local(inputs, leaf_maps, transfer_blocks):
    nodes, _, depth, columns = inputs.shape
    rank = leaf_maps.shape[2]
    levels = transfer_blocks.shape[0]
    chunks = columns // LANES
    units = nodes * chunks
    src_bits = lax.axis_size("src").bit_length() - 1
    tgt_bits = lax.axis_size("tgt").bit_length() - 1
    maps = leaf_maps.reshape(nodes, 2 * rank, depth)
    blocks = transfer_blocks.reshape(levels, nodes, 2, 2 * rank, rank)
    unit = pltpu.VMEM((units, rank, 2 * LANES), jnp.bfloat16)
    dma = pltpu.SemaphoreType.DMA
    return pl.pallas_call(
        functools.partial(kernel, (src_bits, tgt_bits, levels, chunks)),
        out_shape=jax.ShapeDtypeStruct((nodes, 2, rank, columns), jnp.bfloat16),
        in_specs=[pl.BlockSpec(memory_space=pl.ANY)] * 3,
        out_specs=pl.BlockSpec(memory_space=pl.ANY),
        scratch_shapes=[
            pltpu.VMEM((chunks, nodes, depth, 2 * LANES), jnp.bfloat16),
            pltpu.VMEM(maps.shape, jnp.bfloat16),
            pltpu.VMEM(blocks.shape, jnp.bfloat16),
            unit,
            pltpu.VMEM((units, rank, 2 * LANES), jnp.float32),
        ]
        + [unit] * 7
        + [
            dma((chunks, nodes, 2)),
            dma((nodes,)),
            dma((levels,)),
            dma((units, 2)),
        ]
        + [dma((units,))] * 6,
        compiler_params=pltpu.CompilerParams(
            collective_id=0, has_side_effects=True, vmem_limit_bytes=60 * 2**20
        ),
    )(inputs, maps, blocks)


def solution(mesh):
    placed = (
        P(("src", "tgt"), None, None, None),
        P(("src", "tgt"), None, None, None),
        P(None, ("src", "tgt"), None, None, None, None),
    )
    return jax.shard_map(
        local,
        mesh=mesh,
        in_specs=placed,
        out_specs=P(("src", "tgt"), None, None, None),
        check_vma=False,
    )
```

```python
import functools

import jax
import jax.numpy as jnp
from jax import lax
from jax.experimental import pallas as pl
from jax.experimental.pallas import tpu as pltpu
from jax.sharding import PartitionSpec as P

MESH = pl.DeviceIdType.MESH
LANES = 128
HALF = LANES // 2
AHEAD = 4
LIMIT = 60
LEAD = 4
LAG2 = 3
LAG3 = 2


def low_lanes(shape):
    return lax.broadcasted_iota(jnp.int32, shape, 1) < HALF


def times_i(slot):
    turned = pltpu.roll(slot, HALF, 1)
    return jnp.where(low_lanes(slot.shape), -turned, turned)


def stacked(slot):
    rounded = slot.astype(jnp.bfloat16)
    return jnp.concatenate([rounded, times_i(slot).astype(jnp.bfloat16)], axis=0)


def dot(left, right):
    return jnp.dot(left, right, preferred_element_type=jnp.float32)


def kernel(
    sizes,
    inputs,
    leaf_maps,
    transfer,
    out,
    x_in,
    maps,
    blocks,
    vectors,
    coeffs,
    local_term,
    send1,
    recv1,
    send2,
    recv2,
    send3,
    recv3,
    in_sem,
    maps_sem,
    blocks_sem,
    s1_sem,
    r1_sem,
    s2_sem,
    r2_sem,
    s3_sem,
    r3_sem,
):
    src_bits, tgt_bits, levels, chunks = sizes
    items = 4 * chunks
    rank = maps.shape[1] // 2
    src, tgt = lax.axis_index("src"), lax.axis_index("tgt")
    hi, lo = 2 ** (src_bits - 1), 2 ** (src_bits - 2)
    far = 2 ** (tgt_bits - 1)
    bit1, bit2, bit3 = src // hi % 2, src // lo % 2, tgt // far % 2
    across = (src + hi - 2 * hi * bit1, tgt)
    near = (src + lo - 2 * lo * bit2, tgt)
    side = (src, tgt + far - 2 * far * bit3)
    is_end = bit1 == bit2
    is_mid = bit1 != bit2

    barrier = pltpu.get_barrier_semaphore()
    for peer in (across, near, side):
        pl.semaphore_signal(barrier, inc=1, device_id=peer, device_id_type=MESH)

    def load_in(c, n, part):
        return pltpu.make_async_copy(
            inputs.at[n, part, :, pl.ds(pl.multiple_of(c * LANES, LANES), LANES)],
            x_in.at[c, n, :, pl.ds(part * LANES, LANES)],
            in_sem.at[c, n, part],
        )

    def load_maps(n):
        return pltpu.make_async_copy(leaf_maps.at[n], maps.at[n], maps_sem.at[n])

    def load_blocks(v, k, part):
        return pltpu.make_async_copy(
            transfer.at[v, :, k, part],
            blocks.at[v, :, k, :, pl.ds(part * rank, rank)],
            blocks_sem.at[v, k, part],
        )

    def start_in(c):
        for n in range(2):
            for part in range(2):
                load_in(c, n, part).start()

    def start_blocks(v, k):
        for part in range(2):
            load_blocks(v, k, part).start()

    def wait_blocks(v, k):
        for part in range(2):
            load_blocks(v, k, part).wait()

    for n in range(2):
        load_maps(n).start()
        for part in range(2):
            load_in(0, n, part).start()
    for k in range(2):
        start_blocks(0, k)
    start_blocks(1, 1 - bit1)

    def remote(source, target, send_sem, recv_sem, peer):
        return pltpu.make_async_remote_copy(
            src_ref=source,
            dst_ref=target,
            send_sem=send_sem,
            recv_sem=recv_sem,
            device_id=peer,
            device_id_type=MESH,
        )

    def first(i):
        return remote(send1.at[i], recv1.at[i], s1_sem.at[i], r1_sem.at[i], across)

    def second(i):
        return remote(send2.at[i], recv2.at[i], s2_sem.at[i], r2_sem.at[i], near)

    def third(i):
        return remote(send3.at[i], recv3.at[i], s3_sem.at[i], r3_sem.at[i], side)

    def leaf(c, n):
        both = dot(maps[n], x_in[c, n])
        real_part = both[:rank, :LANES] - both[rank:, LANES:]
        imag_part = both[:rank, LANES:] + both[rank:, :LANES]
        low = low_lanes(real_part.shape)
        slots = (
            jnp.where(low, real_part, pltpu.roll(imag_part, HALF, 1)),
            jnp.where(low, pltpu.roll(real_part, HALF, 1), imag_part),
        )
        return jnp.concatenate([stacked(slot) for slot in slots], axis=1)

    def leaves(c):
        for n in range(2):

            @pl.when(c == 0)
            def _():
                load_maps(n).wait()

            for part in range(2):
                load_in(c, n, part).wait()

            @pl.when(c == 0)
            def _():
                start_in(n + 1)

            vectors[n] = leaf(c, n)

    def spread(c):
        @pl.when(c == 0)
        def _():
            for k in range(2):
                wait_blocks(0, k)
            start_blocks(1, bit1)
            for v in range(2, levels):
                for k in range(2):
                    start_blocks(v, k)
            for w in range(3, chunks):
                start_in(w)
            wait_blocks(1, 1 - bit1)

        for n in range(2):
            updated = dot(blocks[0, n, n], vectors[n]) + dot(
                blocks[0, 1 - n, n], vectors[1 - n]
            )
            slots = [
                stacked(updated[:, h * LANES : (h + 1) * LANES]) for h in range(2)
            ]
            sent = dot(
                blocks[1, n, 1 - bit1], jnp.concatenate(slots, axis=1)
            ).astype(jnp.bfloat16)
            for h in range(2):
                i = 4 * c + 2 * n + h
                coeffs[i] = slots[h]
                send1[i] = sent[:, h * LANES : (h + 1) * LANES]
            for h in range(2):
                i = 4 * c + 2 * n + h

                @pl.when(jnp.logical_or(is_mid, i < AHEAD))
                def _():
                    first(i).start()

    def one(i):
        n = i // 2 % 2
        own = dot(blocks[1, n, bit1], coeffs[i])
        first(i).wait_recv()
        slot = stacked(own + recv1[i].astype(jnp.float32))
        send2[i] = dot(blocks[2, n, 1 - bit2], slot).astype(jnp.bfloat16)
        second(i).start()

        local_term[i] = dot(blocks[2, n, bit2], slot)

    def two(i):
        n = i // 2 % 2
        second(i).wait_recv()
        slot = stacked(local_term[i] + recv2[i].astype(jnp.float32))
        send3[i] = dot(blocks[3, n, 1 - bit3], slot).astype(jnp.bfloat16)
        third(i).start()
        local_term[i] = dot(blocks[3, n, bit3], slot)

    def three(j):
        slots = []
        for h in range(2):
            i = 2 * j + h
            third(i).wait_recv()
            slots.append(local_term[i] + recv3[i].astype(jnp.float32))
        low = low_lanes(slots[0].shape)
        real_part = jnp.where(low, slots[0], pltpu.roll(slots[1], HALF, 1))
        imag_part = jnp.where(low, pltpu.roll(slots[0], HALF, 1), slots[1])
        columns = pl.ds(pl.multiple_of(j // 2 * LANES, LANES), LANES)
        out[j % 2, 0, :, columns] = real_part.astype(jnp.bfloat16)
        out[j % 2, 1, :, columns] = imag_part.astype(jnp.bfloat16)

    pl.semaphore_wait(barrier, 3)

    @pl.loop(0, items + LEAD + LAG2 + LAG3)
    def _(t):
        i = t - LEAD

        @pl.when(jnp.logical_and(i >= 0, i < items))
        def _():
            one(i)

        @pl.when(jnp.logical_and(t % 2 == 0, t < 2 * chunks))
        def _():
            leaves(t // 2)

        @pl.when(jnp.logical_and(t % 2 == 1, t < 2 * chunks))
        def _():
            spread(t // 2)

        ahead = i + AHEAD

        @pl.when(jnp.logical_and(is_end, jnp.logical_and(i >= 0, ahead < items)))
        def _():
            first(ahead).start()

        @pl.when(t == 1)
        def _():
            wait_blocks(1, bit1)
            for v in range(2, levels):
                for k in range(2):
                    wait_blocks(v, k)

        @pl.when(jnp.logical_and(i >= LAG2, i < items + LAG2))
        def _():
            two(i - LAG2)

        done = i - LAG2 - LAG3

        @pl.when(jnp.logical_and(done >= 0, done % 2 == 1))
        def _():
            three(done // 2)

    @pl.loop(0, items)
    def _(i):
        first(i).wait_send()
        second(i).wait_send()
        third(i).wait_send()


def local(inputs, leaf_maps, transfer_blocks):
    nodes, _, depth, columns = inputs.shape
    rank = leaf_maps.shape[2]
    levels = transfer_blocks.shape[0]
    chunks = columns // LANES
    items = 2 * nodes * chunks
    src_bits = lax.axis_size("src").bit_length() - 1
    tgt_bits = lax.axis_size("tgt").bit_length() - 1
    maps = leaf_maps.reshape(nodes, 2 * rank, depth)
    slots = pltpu.VMEM((items, rank, LANES), jnp.bfloat16)
    dma = pltpu.SemaphoreType.DMA
    return pl.pallas_call(
        functools.partial(kernel, (src_bits, tgt_bits, levels, chunks)),
        out_shape=pltpu.VMEM((nodes, 2, rank, columns), jnp.bfloat16),
        in_specs=[pl.BlockSpec(memory_space=pl.ANY)] * 3,
        out_specs=pl.BlockSpec(memory_space=pltpu.VMEM),
        scratch_shapes=[
            pltpu.VMEM((chunks, nodes, depth, 2 * LANES), jnp.bfloat16),
            pltpu.VMEM(maps.shape, jnp.bfloat16),
            pltpu.VMEM((levels, nodes, 2, rank, 2 * rank), jnp.bfloat16),
            pltpu.VMEM((nodes, 2 * rank, 2 * LANES), jnp.bfloat16),
            pltpu.VMEM((items, 2 * rank, LANES), jnp.bfloat16),
            pltpu.VMEM((items, rank, LANES), jnp.float32),
        ]
        + [slots] * 6
        + [
            dma((chunks, nodes, 2)),
            dma((nodes,)),
            dma((levels, 2, 2)),
        ]
        + [dma((items,))] * 6,
        compiler_params=pltpu.CompilerParams(
            collective_id=0, has_side_effects=True, vmem_limit_bytes=LIMIT * 2**20
        ),
    )(inputs, maps, transfer_blocks)


def solution(mesh):
    placed = (
        P(("src", "tgt"), None, None, None),
        P(("src", "tgt"), None, None, None),
        P(None, ("src", "tgt"), None, None, None, None),
    )
    return jax.shard_map(
        local,
        mesh=mesh,
        in_specs=placed,
        out_specs=P(("src", "tgt"), None, None, None),
        check_vma=False,
    )
```

```python
import functools

import jax
import jax.numpy as jnp
from jax import lax
from jax.experimental import pallas as pl
from jax.experimental.pallas import tpu as pltpu
from jax.sharding import PartitionSpec as P

MESH = pl.DeviceIdType.MESH
LANES = 128
HALF = LANES // 2
AHEAD = 4
LIMIT = 60
LEAD = 4
LAG2 = 3
LAG3 = 2


def low_lanes(shape):
    return lax.broadcasted_iota(jnp.int32, shape, 1) < HALF


def times_i(slot):
    turned = pltpu.roll(slot, HALF, 1)
    return jnp.where(low_lanes(slot.shape), -turned, turned)


def stacked(slot):
    rounded = slot.astype(jnp.bfloat16)
    return jnp.concatenate([rounded, times_i(slot).astype(jnp.bfloat16)], axis=0)


def dot(left, right):
    return jnp.dot(left, right, preferred_element_type=jnp.float32)


def kernel(
    sizes,
    inputs,
    leaf_maps,
    transfer,
    out,
    x_in,
    maps,
    mix,
    blocks,
    vectors,
    local_term,
    send1,
    recv1,
    send2,
    recv2,
    send3,
    recv3,
    in_sem,
    maps_sem,
    mix_sem,
    blocks_sem,
    s1_sem,
    r1_sem,
    s2_sem,
    r2_sem,
    s3_sem,
    r3_sem,
):
    src_bits, tgt_bits, levels, chunks = sizes
    items = 4 * chunks
    rank = maps.shape[1] // 2
    src, tgt = lax.axis_index("src"), lax.axis_index("tgt")
    hi, lo = 2 ** (src_bits - 1), 2 ** (src_bits - 2)
    far = 2 ** (tgt_bits - 1)
    bit1, bit2, bit3 = src // hi % 2, src // lo % 2, tgt // far % 2
    across = (src + hi - 2 * hi * bit1, tgt)
    near = (src + lo - 2 * lo * bit2, tgt)
    side = (src, tgt + far - 2 * far * bit3)
    is_end = bit1 == bit2
    is_mid = bit1 != bit2

    barrier = pltpu.get_barrier_semaphore()
    for peer in (across, near, side):
        pl.semaphore_signal(barrier, inc=1, device_id=peer, device_id_type=MESH)

    def load_in(c, n, part):
        return pltpu.make_async_copy(
            inputs.at[n, part, :, pl.ds(pl.multiple_of(c * LANES, LANES), LANES)],
            x_in.at[c, n, :, pl.ds(part * LANES, LANES)],
            in_sem.at[c, n, part],
        )

    def load_maps(n):
        return pltpu.make_async_copy(leaf_maps.at[n], maps.at[n], maps_sem.at[n])

    def load_mix(m, part):
        return pltpu.make_async_copy(
            transfer.at[0, m, :, part],
            mix.at[:, :, pl.ds((2 * m + part) * rank, rank)],
            mix_sem.at[m, part],
        )

    def load_blocks(v, k, part):
        bit = (bit1, bit2, bit3)[v]
        return pltpu.make_async_copy(
            transfer.at[v + 1, :, bit if k else 1 - bit, part],
            blocks.at[v, :, k, :, pl.ds(part * rank, rank)],
            blocks_sem.at[v, k, part],
        )

    def start_in(c):
        for n in range(2):
            for part in range(2):
                load_in(c, n, part).start()

    def start_blocks(v, k):
        for part in range(2):
            load_blocks(v, k, part).start()

    def wait_blocks(v, k):
        for part in range(2):
            load_blocks(v, k, part).wait()

    for n in range(2):
        load_maps(n).start()
        for part in range(2):
            load_in(0, n, part).start()
    for m in range(2):
        for part in range(2):
            load_mix(m, part).start()
    for k in range(2):
        start_blocks(0, k)

    def remote(source, target, send_sem, recv_sem, peer):
        return pltpu.make_async_remote_copy(
            src_ref=source,
            dst_ref=target,
            send_sem=send_sem,
            recv_sem=recv_sem,
            device_id=peer,
            device_id_type=MESH,
        )

    def first(i):
        return remote(send1.at[i], recv1.at[i], s1_sem.at[i], r1_sem.at[i], across)

    def second(i):
        return remote(send2.at[i], recv2.at[i], s2_sem.at[i], r2_sem.at[i], near)

    def third(i):
        return remote(send3.at[i], recv3.at[i], s3_sem.at[i], r3_sem.at[i], side)

    def leaf(c, n):
        both = dot(maps[n], x_in[c, n])
        real_part = both[:rank, :LANES] - both[rank:, LANES:]
        imag_part = both[:rank, LANES:] + both[rank:, :LANES]
        low = low_lanes(real_part.shape)
        real_turned = pltpu.roll(real_part, HALF, 1)
        imag_turned = pltpu.roll(imag_part, HALF, 1)
        slots = (
            jnp.where(low, real_part, imag_turned),
            jnp.where(low, real_turned, imag_part),
        )
        turned = (
            jnp.where(low, -imag_part, real_turned),
            jnp.where(low, -imag_turned, real_part),
        )
        return jnp.concatenate(
            [
                jnp.concatenate([part.astype(jnp.bfloat16) for part in both], axis=1)
                for both in (slots, turned)
            ],
            axis=0,
        )

    def leaves(c):
        for n in range(2):

            @pl.when(c == 0)
            def _():
                load_maps(n).wait()

            for part in range(2):
                load_in(c, n, part).wait()

            @pl.when(c == 0)
            def _():
                start_in(n + 1)

            vectors[pl.ds(2 * rank * n, 2 * rank)] = leaf(c, n)

    def spread(c):
        @pl.when(c == 0)
        def _():
            for m in range(2):
                for part in range(2):
                    load_mix(m, part).wait()
            for v in range(1, levels - 1):
                for k in range(2):
                    start_blocks(v, k)
            for w in range(3, chunks):
                start_in(w)
            wait_blocks(0, 0)

        for n in range(2):
            updated = dot(mix[n], vectors[...])
            slots = jnp.concatenate(
                [stacked(updated[:, h * LANES : (h + 1) * LANES]) for h in range(2)],
                axis=1,
            )
            sent = dot(blocks[0, n, 0], slots).astype(jnp.bfloat16)
            for h in range(2):
                i = 4 * c + 2 * n + h
                send1[i] = sent[:, h * LANES : (h + 1) * LANES]

                @pl.when(jnp.logical_or(is_mid, i < AHEAD))
                def _():
                    first(i).start()

            if n == 0:

                @pl.when(c == 0)
                def _():
                    wait_blocks(0, 1)

            own = dot(blocks[0, n, 1], slots)
            for h in range(2):
                local_term[4 * c + 2 * n + h] = own[:, h * LANES : (h + 1) * LANES]

    def one(i):
        n = i // 2 % 2
        first(i).wait_recv()
        slot = stacked(local_term[i] + recv1[i].astype(jnp.float32))
        send2[i] = dot(blocks[1, n, 0], slot).astype(jnp.bfloat16)
        second(i).start()
        local_term[i] = dot(blocks[1, n, 1], slot)

    def two(i):
        n = i // 2 % 2
        second(i).wait_recv()
        slot = stacked(local_term[i] + recv2[i].astype(jnp.float32))
        send3[i] = dot(blocks[2, n, 0], slot).astype(jnp.bfloat16)
        third(i).start()
        local_term[i] = dot(blocks[2, n, 1], slot)

    def three(j):
        slots = []
        for h in range(2):
            i = 2 * j + h
            third(i).wait_recv()
            slots.append(local_term[i] + recv3[i].astype(jnp.float32))
        low = low_lanes(slots[0].shape)
        real_part = jnp.where(low, slots[0], pltpu.roll(slots[1], HALF, 1))
        imag_part = jnp.where(low, pltpu.roll(slots[0], HALF, 1), slots[1])
        columns = pl.ds(pl.multiple_of(j // 2 * LANES, LANES), LANES)
        out[j % 2, 0, :, columns] = real_part.astype(jnp.bfloat16)
        out[j % 2, 1, :, columns] = imag_part.astype(jnp.bfloat16)

    pl.semaphore_wait(barrier, 3)

    @pl.loop(0, items + LEAD + LAG2 + LAG3)
    def _(t):
        i = t - LEAD

        @pl.when(jnp.logical_and(i >= 0, i < items))
        def _():
            one(i)

        @pl.when(jnp.logical_and(t % 2 == 0, t < 2 * chunks))
        def _():
            leaves(t // 2)

        @pl.when(jnp.logical_and(t % 2 == 1, t < 2 * chunks))
        def _():
            spread(t // 2)

        ahead = i + AHEAD

        @pl.when(jnp.logical_and(is_end, jnp.logical_and(i >= 0, ahead < items)))
        def _():
            first(ahead).start()

        @pl.when(t == 1)
        def _():
            for v in range(1, levels - 1):
                for k in range(2):
                    wait_blocks(v, k)

        @pl.when(jnp.logical_and(i >= LAG2, i < items + LAG2))
        def _():
            two(i - LAG2)

        done = i - LAG2 - LAG3

        @pl.when(jnp.logical_and(done >= 0, done % 2 == 1))
        def _():
            three(done // 2)

    @pl.loop(0, items)
    def _(i):
        first(i).wait_send()
        second(i).wait_send()
        third(i).wait_send()


def local(inputs, leaf_maps, transfer_blocks):
    nodes, _, depth, columns = inputs.shape
    rank = leaf_maps.shape[2]
    levels = transfer_blocks.shape[0]
    chunks = columns // LANES
    items = 2 * nodes * chunks
    src_bits = lax.axis_size("src").bit_length() - 1
    tgt_bits = lax.axis_size("tgt").bit_length() - 1
    maps = leaf_maps.reshape(nodes, 2 * rank, depth)
    slots = pltpu.VMEM((items, rank, LANES), jnp.bfloat16)
    dma = pltpu.SemaphoreType.DMA
    return pl.pallas_call(
        functools.partial(kernel, (src_bits, tgt_bits, levels, chunks)),
        out_shape=pltpu.VMEM((nodes, 2, rank, columns), jnp.bfloat16),
        in_specs=[pl.BlockSpec(memory_space=pl.ANY)] * 3,
        out_specs=pl.BlockSpec(memory_space=pltpu.VMEM),
        scratch_shapes=[
            pltpu.VMEM((chunks, nodes, depth, 2 * LANES), jnp.bfloat16),
            pltpu.VMEM(maps.shape, jnp.bfloat16),
            pltpu.VMEM((nodes, rank, 2 * nodes * rank), jnp.bfloat16),
            pltpu.VMEM((levels - 1, nodes, 2, rank, 2 * rank), jnp.bfloat16),
            pltpu.VMEM((2 * nodes * rank, 2 * LANES), jnp.bfloat16),
            pltpu.VMEM((items, rank, LANES), jnp.float32),
        ]
        + [slots] * 6
        + [
            dma((chunks, nodes, 2)),
            dma((nodes,)),
            dma((nodes, 2)),
            dma((levels - 1, 2, 2)),
        ]
        + [dma((items,))] * 6,
        compiler_params=pltpu.CompilerParams(
            collective_id=0, has_side_effects=True, vmem_limit_bytes=LIMIT * 2**20
        ),
    )(inputs, maps, transfer_blocks)


def solution(mesh):
    placed = (
        P(("src", "tgt"), None, None, None),
        P(("src", "tgt"), None, None, None),
        P(None, ("src", "tgt"), None, None, None, None),
    )
    return jax.shard_map(
        local,
        mesh=mesh,
        in_specs=placed,
        out_specs=P(("src", "tgt"), None, None, None),
        check_vma=False,
    )
```

```python
import functools

import jax
import jax.numpy as jnp
from jax import lax
from jax.experimental import pallas as pl
from jax.experimental.pallas import tpu as pltpu
from jax.sharding import PartitionSpec as P

MESH = pl.DeviceIdType.MESH
LANES = 128
HALF = LANES // 2
AHEAD = 4
LIMIT = 60
LEAD = 3
LAG2 = 3
LAG3 = 2


def low_lanes(shape):
    return lax.broadcasted_iota(jnp.int32, shape, 1) < HALF


def times_i(slot):
    turned = pltpu.roll(slot, HALF, 1)
    return jnp.where(low_lanes(slot.shape), -turned, turned)


def stacked(slot):
    rounded = slot.astype(jnp.bfloat16)
    return jnp.concatenate([rounded, times_i(slot).astype(jnp.bfloat16)], axis=0)


def dot(left, right):
    return jnp.dot(left, right, preferred_element_type=jnp.float32)


def kernel(
    sizes,
    inputs,
    leaf_maps,
    transfer,
    out,
    x_in,
    maps,
    mix,
    blocks,
    vectors,
    local_term,
    send1,
    recv1,
    send2,
    recv2,
    send3,
    recv3,
    in_sem,
    maps_sem,
    mix_sem,
    blocks_sem,
    s1_sem,
    r1_sem,
    s2_sem,
    r2_sem,
    s3_sem,
    r3_sem,
):
    src_bits, tgt_bits, levels, chunks = sizes
    items = 4 * chunks
    rank = maps.shape[1] // 2
    src, tgt = lax.axis_index("src"), lax.axis_index("tgt")
    hi, lo = 2 ** (src_bits - 1), 2 ** (src_bits - 2)
    far = 2 ** (tgt_bits - 1)
    bit1, bit2, bit3 = src // hi % 2, src // lo % 2, tgt // far % 2
    across = (src + hi - 2 * hi * bit1, tgt)
    near = (src + lo - 2 * lo * bit2, tgt)
    side = (src, tgt + far - 2 * far * bit3)
    is_end = bit1 == bit2
    is_mid = bit1 != bit2

    barrier = pltpu.get_barrier_semaphore()
    for peer in (across, near, side):
        pl.semaphore_signal(barrier, inc=1, device_id=peer, device_id_type=MESH)

    def load_in(c, n, part):
        return pltpu.make_async_copy(
            inputs.at[n, part, :, pl.ds(pl.multiple_of(c * LANES, LANES), LANES)],
            x_in.at[c, n, :, pl.ds(part * LANES, LANES)],
            in_sem.at[c, n, part],
        )

    def load_maps(n):
        return pltpu.make_async_copy(leaf_maps.at[n], maps.at[n], maps_sem.at[n])

    def load_mix(m, part):
        return pltpu.make_async_copy(
            transfer.at[0, m, :, part],
            mix.at[:, :, pl.ds((2 * m + part) * rank, rank)],
            mix_sem.at[m, part],
        )

    def load_blocks(v, k, part):
        bit = (bit1, bit2, bit3)[v]
        return pltpu.make_async_copy(
            transfer.at[v + 1, :, bit if k else 1 - bit, part],
            blocks.at[v, :, k, :, pl.ds(part * rank, rank)],
            blocks_sem.at[v, k, part],
        )

    def start_in(c):
        for n in range(2):
            for part in range(2):
                load_in(c, n, part).start()

    def start_blocks(v, k):
        for part in range(2):
            load_blocks(v, k, part).start()

    def wait_blocks(v, k):
        for part in range(2):
            load_blocks(v, k, part).wait()

    for n in range(2):
        for part in range(2):
            load_in(0, n, part).start()
        load_maps(n).start()
    for m in range(2):
        for part in range(2):
            load_mix(m, part).start()
    for k in range(2):
        start_blocks(0, k)

    def remote(source, target, send_sem, recv_sem, peer):
        return pltpu.make_async_remote_copy(
            src_ref=source,
            dst_ref=target,
            send_sem=send_sem,
            recv_sem=recv_sem,
            device_id=peer,
            device_id_type=MESH,
        )

    def first(i):
        return remote(send1.at[i], recv1.at[i], s1_sem.at[i], r1_sem.at[i], across)

    def second(i):
        return remote(send2.at[i], recv2.at[i], s2_sem.at[i], r2_sem.at[i], near)

    def third(i):
        return remote(send3.at[i], recv3.at[i], s3_sem.at[i], r3_sem.at[i], side)

    def leaf(c, n):
        both = dot(maps[n], x_in[c, n])
        real_part = both[:rank, :LANES] - both[rank:, LANES:]
        imag_part = both[:rank, LANES:] + both[rank:, :LANES]
        low = low_lanes(real_part.shape)
        real_turned = pltpu.roll(real_part, HALF, 1)
        imag_turned = pltpu.roll(imag_part, HALF, 1)
        slots = (
            jnp.where(low, real_part, imag_turned),
            jnp.where(low, real_turned, imag_part),
        )
        turned = (
            jnp.where(low, -imag_part, real_turned),
            jnp.where(low, -imag_turned, real_part),
        )
        return jnp.concatenate(
            [
                jnp.concatenate([part.astype(jnp.bfloat16) for part in both], axis=1)
                for both in (slots, turned)
            ],
            axis=0,
        )

    def leaves(c):
        for n in range(2):

            @pl.when(c == 0)
            def _():
                load_maps(n).wait()

            for part in range(2):
                load_in(c, n, part).wait()

            @pl.when(c == 0)
            def _():
                start_in(n + 1)

            vectors[pl.ds(2 * rank * n, 2 * rank)] = leaf(c, n)

    def spread(c):
        @pl.when(c == 0)
        def _():
            for m in range(2):
                for part in range(2):
                    load_mix(m, part).wait()
            for v in range(1, levels - 1):
                for k in range(2):
                    start_blocks(v, k)
            for w in range(3, chunks):
                start_in(w)
            wait_blocks(0, 0)

        for n in range(2):
            updated = dot(mix[n], vectors[...])
            slots = jnp.concatenate(
                [stacked(updated[:, h * LANES : (h + 1) * LANES]) for h in range(2)],
                axis=1,
            )
            sent = dot(blocks[0, n, 0], slots).astype(jnp.bfloat16)
            for h in range(2):
                i = 4 * c + 2 * n + h
                send1[i] = sent[:, h * LANES : (h + 1) * LANES]

                @pl.when(jnp.logical_or(is_mid, i < AHEAD))
                def _():
                    first(i).start()

            if n == 0:

                @pl.when(c == 0)
                def _():
                    wait_blocks(0, 1)

            own = dot(blocks[0, n, 1], slots)
            for h in range(2):
                local_term[4 * c + 2 * n + h] = own[:, h * LANES : (h + 1) * LANES]

    def one(i):
        n = i // 2 % 2
        first(i).wait_recv()
        slot = stacked(local_term[i] + recv1[i].astype(jnp.float32))
        send2[i] = dot(blocks[1, n, 0], slot).astype(jnp.bfloat16)
        second(i).start()
        local_term[i] = dot(blocks[1, n, 1], slot)

    def two(i):
        n = i // 2 % 2
        second(i).wait_recv()
        slot = stacked(local_term[i] + recv2[i].astype(jnp.float32))
        send3[i] = dot(blocks[2, n, 0], slot).astype(jnp.bfloat16)
        third(i).start()
        local_term[i] = dot(blocks[2, n, 1], slot)

    def three(j):
        slots = []
        for h in range(2):
            i = 2 * j + h
            third(i).wait_recv()
            slots.append(local_term[i] + recv3[i].astype(jnp.float32))
        low = low_lanes(slots[0].shape)
        real_part = jnp.where(low, slots[0], pltpu.roll(slots[1], HALF, 1))
        imag_part = jnp.where(low, pltpu.roll(slots[0], HALF, 1), slots[1])
        columns = pl.ds(pl.multiple_of(j // 2 * LANES, LANES), LANES)
        out[j % 2, 0, :, columns] = real_part.astype(jnp.bfloat16)
        out[j % 2, 1, :, columns] = imag_part.astype(jnp.bfloat16)

    pl.semaphore_wait(barrier, 3)

    @pl.loop(0, items + LEAD + LAG2 + LAG3)
    def _(t):
        i = t - LEAD

        @pl.when(jnp.logical_and(i >= 0, i < items))
        def _():
            one(i)

        @pl.when(jnp.logical_and(t % 2 == 0, t < 2 * chunks))
        def _():
            leaves(t // 2)

        @pl.when(jnp.logical_and(t % 2 == 1, t < 2 * chunks))
        def _():
            spread(t // 2)

        ahead = i + AHEAD

        @pl.when(jnp.logical_and(is_end, jnp.logical_and(i >= 0, ahead < items)))
        def _():
            first(ahead).start()

        @pl.when(t == 1)
        def _():
            for v in range(1, levels - 1):
                for k in range(2):
                    wait_blocks(v, k)

        @pl.when(jnp.logical_and(i >= LAG2, i < items + LAG2))
        def _():
            two(i - LAG2)

        done = i - LAG2 - LAG3

        @pl.when(jnp.logical_and(done >= 0, done % 2 == 1))
        def _():
            three(done // 2)

    @pl.loop(0, items)
    def _(i):
        first(i).wait_send()
        second(i).wait_send()
        third(i).wait_send()


def local(inputs, leaf_maps, transfer_blocks):
    nodes, _, depth, columns = inputs.shape
    rank = leaf_maps.shape[2]
    levels = transfer_blocks.shape[0]
    chunks = columns // LANES
    items = 2 * nodes * chunks
    src_bits = lax.axis_size("src").bit_length() - 1
    tgt_bits = lax.axis_size("tgt").bit_length() - 1
    maps = leaf_maps.reshape(nodes, 2 * rank, depth)
    slots = pltpu.VMEM((items, rank, LANES), jnp.bfloat16)
    dma = pltpu.SemaphoreType.DMA
    return pl.pallas_call(
        functools.partial(kernel, (src_bits, tgt_bits, levels, chunks)),
        out_shape=pltpu.VMEM((nodes, 2, rank, columns), jnp.bfloat16),
        in_specs=[pl.BlockSpec(memory_space=pl.ANY)] * 3,
        out_specs=pl.BlockSpec(memory_space=pltpu.VMEM),
        scratch_shapes=[
            pltpu.VMEM((chunks, nodes, depth, 2 * LANES), jnp.bfloat16),
            pltpu.VMEM(maps.shape, jnp.bfloat16),
            pltpu.VMEM((nodes, rank, 2 * nodes * rank), jnp.bfloat16),
            pltpu.VMEM((levels - 1, nodes, 2, rank, 2 * rank), jnp.bfloat16),
            pltpu.VMEM((2 * nodes * rank, 2 * LANES), jnp.bfloat16),
            pltpu.VMEM((items, rank, LANES), jnp.float32),
        ]
        + [slots] * 6
        + [
            dma((chunks, nodes, 2)),
            dma((nodes,)),
            dma((nodes, 2)),
            dma((levels - 1, 2, 2)),
        ]
        + [dma((items,))] * 6,
        compiler_params=pltpu.CompilerParams(
            collective_id=0, has_side_effects=True, vmem_limit_bytes=LIMIT * 2**20
        ),
    )(inputs, maps, transfer_blocks)


def solution(mesh):
    placed = (
        P(("src", "tgt"), None, None, None),
        P(("src", "tgt"), None, None, None),
        P(None, ("src", "tgt"), None, None, None, None),
    )
    return jax.shard_map(
        local,
        mesh=mesh,
        in_specs=placed,
        out_specs=P(("src", "tgt"), None, None, None),
        check_vma=False,
    )
```
